32 devices in a mesh: seq: 8 (over z, y), chan: 2 (over x), section: 2 (over core).
Axes of the slice: x: 2, y: 2, z: 4, core: 2. Of those that a mesh axis runs over, the one named last changes fastest.
Arguments:
- tokens: bfloat16 [2, 2048, 1024], P(None, 'seq', 'chan'), may hold values from -6 to 6
- in_proj: bfloat16 [2, 1024, 2, 1024], P('section', None, None, 'chan'), may hold values from -0.1875 to 0.1875
- filters: bfloat16 [2, 8, 2304], P('section', 'chan'), may hold values from -0.13183594 to 0.13183594
- out_proj: bfloat16 [2, 1024, 1024], P('section', None, 'chan'), may hold values from -0.1875 to 0.1875
- widths: int32 [2], replicated, may hold values from 1 to 4, as said below
Outputs:
- layer_outputs: bfloat16 [2, 2, 2048, 1024], P('section', None, 'seq', 'chan')
The draws below stay inside these ranges and needn't reach their ends.
Inputs may be any that keep to these rules, and one draw needn't show every extreme that they name: `widths`: exactly one sequence has width 8 / 2.
All inputs are finite; a program needn't handle non-finite values.
Results may differ from the reference program's by a relative error of at most 0.0077.
Values may be sent and summed in bfloat16 or wider, within the bound.
No kernel may reach another device: no remote copies, remote signals or barrier semaphores. Data moves between devices by JAX's collectives and lax.ppermute only.
A program may use at most 64 MiB of HBM per device.

```python
import jax
import jax.numpy as jnp
import numpy as np
from jax import lax

D = 1024
HEADS = 8
BLK = 256
BAND = 8
MB = 2
HD = 128
TAPS = 2304
NB = 8
LEN = 2048
LAYERS = 2


def draw_widths(key, part):
    keys = jax.random.split(jax.random.fold_in(key, 11), 2)
    band_widths = jax.random.randint(keys[0], (MB,), 1, BAND // 2)
    chosen = jax.random.randint(keys[1], (), 0, MB)
    band_widths = jnp.where(jnp.arange(MB) == chosen, BAND // 2, band_widths)
    return band_widths.astype(jnp.int32)


def block_levels(rng, extent, pieces, least, largest):
    factor_of, own = 1.0, jax.random.fold_in(rng, 6)
    for axis_at, parts in pieces:
        steps = jnp.exp(jax.random.uniform(jax.random.fold_in(own, axis_at), (parts,), jnp.float32, least / len(pieces), largest / len(pieces)))
        factor_of = factor_of * jnp.repeat(steps, extent[axis_at] // parts).reshape([-1 if axis == axis_at else 1 for axis in range(len(extent))])
    return factor_of


def bell_draw(rng, shape, width, most, cuts=(), kind=jnp.bfloat16):
    array = jax.random.normal(rng, shape, jnp.float32) * width
    if len(cuts) > 0:
        array = block_levels(rng, shape, cuts, -0.22, 0.18) * array
    return jnp.clip(array, min=-most, max=most).astype(kind)


def setup_inputs(seed: int = 0) -> dict:
    key_list = jax.random.split(jax.random.key(seed), 6)
    tokens = bell_draw(key_list[0], (MB, LEN, D), 1.0, 6.0, ((1, 8), (2, 2)))
    in_proj = bell_draw(key_list[1], (LAYERS, D, 2, D), D ** -0.5, 0.1875, ((0, 2), (3, 2)))
    filters = bell_draw(key_list[2], (LAYERS, HEADS, TAPS), (1.0 / (BAND * BLK) ** 0.5), 0.13183594, ((0, 2), (1, 2)))
    out_proj = bell_draw(key_list[3], (LAYERS, D, D), D ** -0.5, 0.1875, ((0, 2), (2, 2)))
    widths = draw_widths(jax.random.fold_in(key_list[5], 71), 0)
    return dict(tokens=tokens, in_proj=in_proj, filters=filters, out_proj=out_proj, widths=widths)


def layer_apply(layer_input, input_weight, taps, output_weight, band_width):
    projected = jnp.dot(layer_input, input_weight.reshape(D, 2 * D), preferred_element_type=jnp.float32)
    projected = projected.reshape(LEN, 2, D)
    signal = projected[:, 0, :].astype(jnp.bfloat16)
    gating = projected[:, 1, :].astype(jnp.bfloat16)
    blocks = signal.reshape(NB, BLK, HEADS, HD).astype(jnp.float32)
    reach = BAND // 2
    positions = np.arange(BLK)
    mixed = jnp.zeros((NB, BLK, HEADS, HD), jnp.float32)
    for block_lag in range(-reach, reach):
        table = BLK * block_lag + positions[:, None] - positions[None, :] + (reach + 1) * BLK
        matrices = taps[:, table].astype(jnp.float32)
        source = jnp.roll(blocks, block_lag, axis=0)
        in_band = ((block_lag >= -band_width) & (block_lag < band_width)).astype(jnp.float32)
        product = jnp.einsum("hts,ishc->ithc", matrices, source, precision=lax.Precision.HIGHEST)
        mixed = mixed + in_band * product
    gated = (jax.nn.silu(gating.astype(jnp.float32)) * mixed.reshape(LEN, D)).astype(jnp.bfloat16)
    return jnp.dot(gated, output_weight, preferred_element_type=jnp.float32).astype(jnp.bfloat16)


def reference(tokens, in_proj, filters, out_proj, widths):
    per_layer = [[] for layer_index in range(LAYERS)]
    for batch_index in range(MB):
        current = tokens[batch_index]
        for layer_index in range(LAYERS):
            current = layer_apply(current, in_proj[layer_index], filters[layer_index], out_proj[layer_index], widths[batch_index])
            per_layer[layer_index].append(current)
    return jnp.stack([jnp.stack(outputs) for outputs in per_layer])
```

```python
import functools

import jax
import jax.numpy as jnp
from jax import lax
from jax.experimental import pallas as pl
from jax.experimental.pallas import tpu as pltpu
from jax.sharding import PartitionSpec as P

BAND = 8
REACH = BAND // 2
MB = 2


VMEM = pl.BlockSpec(memory_space=pltpu.VMEM)
SMEM = pl.BlockSpec(memory_space=pltpu.SMEM)


def call(kernel, outs, specs, name, flops, moved):
    return pl.pallas_call(
        kernel,
        out_shape=outs,
        in_specs=specs,
        out_specs=jax.tree.map(lambda _: VMEM, outs),
        name=name,
        cost_estimate=pl.CostEstimate(flops=flops, bytes_accessed=moved, transcendentals=0),
        compiler_params=pltpu.CompilerParams(vmem_limit_bytes=48 << 20),
    )


def shape(*dims):
    return jax.ShapeDtypeStruct(dims, jnp.bfloat16)


def toeplitz_kernel(block, slot_ref, band_ref, taps_ref, out_ref):
    heads, taps = taps_ref.shape
    for head in range(heads):
        row = taps_ref[head : head + 1, :].astype(jnp.float32)
        for at in range(BAND):
            lag = at - REACH
            start = block * (REACH - 1 - lag)
            window = jnp.broadcast_to(row[:, start : start + 2 * block], (block, 2 * block))
            turned = pltpu.roll(window, 1, 1, stride=1, stride_axis=0)[:, block:]
            kept = jnp.where(band_ref[at] > 0, turned, 0.0)
            out_ref[head, slot_ref[at]] = kept.astype(jnp.bfloat16)


def toeplitz(reversed_taps, slot_of_lag, band_of_lag, block):
    heads = reversed_taps.shape[0]
    return call(
        functools.partial(toeplitz_kernel, block),
        shape(heads, BAND, block, block),
        [SMEM, SMEM, VMEM],
        "toeplitz",
        heads * BAND * block * block * 8,
        heads * BAND * block * block * 2,
    )(slot_of_lag, band_of_lag, reversed_taps)


def mix_kernel(toeplitz_ref, gate_ref, *refs):
    sources, out_ref = refs[:-1], refs[-1]
    heads = toeplitz_ref.shape[0]
    wide = gate_ref.shape[1] // heads
    for head in range(heads):
        lanes = pl.ds(head * wide, wide)
        mixed = jnp.dot(toeplitz_ref[head, 0], sources[0][:, lanes], preferred_element_type=jnp.float32)
        for at in range(1, BAND):
            mixed += jnp.dot(toeplitz_ref[head, at], sources[at][:, lanes], preferred_element_type=jnp.float32)
        gate = gate_ref[:, lanes].astype(jnp.float32)
        out_ref[:, lanes] = (gate / (1.0 + jnp.exp(-gate)) * mixed).astype(jnp.bfloat16)


def mix(toeplitz_blocks, gating, sources):
    block, local = gating.shape
    return call(
        mix_kernel,
        shape(block, local),
        [VMEM] * (2 + len(sources)),
        "mix",
        2 * BAND * block * block * local,
        toeplitz_blocks.size * 2 + (len(sources) + 2) * block * local * 2,
    )(toeplitz_blocks, gating, *sources)


def project_kernel(chan_ref, own_ref, peer_ref, weight_ref, *out_refs):
    depth = own_ref.shape[1]
    chan = chan_ref[0]
    own_rows = weight_ref[pl.ds(pl.multiple_of(chan * depth, depth), depth), :]
    peer_rows = weight_ref[pl.ds(pl.multiple_of((1 - chan) * depth, depth), depth), :]
    total = jnp.dot(own_ref[...], own_rows, preferred_element_type=jnp.float32)
    total += jnp.dot(peer_ref[...], peer_rows, preferred_element_type=jnp.float32)
    wide = total.shape[1] // len(out_refs)
    for at, out_ref in enumerate(out_refs):
        out_ref[...] = total[:, at * wide : (at + 1) * wide].astype(jnp.bfloat16)


def project(chan, own, peer, weight, count):
    block, depth = own.shape
    wide = weight.shape[1] // count
    return call(
        project_kernel,
        tuple(shape(block, wide) for _ in range(count)),
        [SMEM, VMEM, VMEM, VMEM],
        "project",
        4 * block * depth * weight.shape[1],
        weight.size * 2 + 2 * own.size * 2 + block * weight.shape[1] * 2,
    )(chan, own, peer, weight)


def per_device(tokens, in_proj, filters, out_proj, widths):
    count = lax.axis_size("seq")
    half = count // 2
    place = lax.axis_index("seq")
    chan = lax.axis_index("chan")
    section = lax.axis_index("section")
    block, local = tokens.shape[1:]
    sequence = (place >= half).astype(jnp.int32)
    index = lax.rem(place + section * half, count)
    chan_scalar = chan.astype(jnp.int32).reshape(1)

    def swap(value, axis):
        return lax.ppermute(value, axis, [(0, 1), (1, 0)])

    def across(value, from_section, to_section):
        pairs = [(2 * i + from_section, 2 * ((i + half) % count) + to_section) for i in range(count)]
        return lax.ppermute(value, ("seq", "section"), pairs)

    def where_held(which, held):
        low = held < half
        if which == 0:
            return (held, 0) if low else (held - half, 1)
        return (held + half, 1) if low else (held, 0)

    def ring(value, lag):
        pairs = []
        for which in range(MB):
            for held in range(count):
                source, target = where_held(which, held), where_held(which, (held + lag) % count)
                pairs.append((2 * source[0] + source[1], 2 * target[0] + target[1]))
        return lax.ppermute(value, ("seq", "section"), pairs)

    own_tokens = lax.dynamic_index_in_dim(tokens, sequence, 0, False)
    other_tokens = lax.dynamic_index_in_dim(tokens, 1 - sequence, 0, False)
    swapped = across(other_tokens, 1, 1)
    current = jnp.where(section == 0, own_tokens, swapped)
    peer = swap(current, "chan")

    def both(value):
        received = swap(value, "section")
        return jnp.where(section == 0, value, received), jnp.where(section == 0, received, value)

    in_weights = both(in_proj[0].reshape(in_proj.shape[1], -1))
    taps = both(filters[0][:, ::-1])
    out_weights = both(out_proj[0])

    lags = jnp.arange(BAND, dtype=jnp.int32) - REACH
    if count == BAND:
        slot_of_lag = index ^ ((index - lags) & (BAND - 1))
    else:
        slot_of_lag = lags + REACH
    band_width = jnp.where(sequence == 0, widths[0], widths[1])
    band_of_lag = ((lags >= -band_width) & (lags < band_width)).astype(jnp.int32)
    blocks = [toeplitz(layer_taps, slot_of_lag, band_of_lag, block) for layer_taps in taps]

    def gather(signal):
        if count != BAND:
            return [ring(signal, lag) if lag else signal for lag in range(-REACH, REACH)]
        near = [signal]
        for step in range(1, REACH):
            near.append(lax.ppermute(signal, "seq", [(i, i ^ step) for i in range(count)]))
        return near + [swap(value, "section") for value in near]

    def gated_of(current, peer, layer):
        signal, gating = project(chan_scalar, current, peer, in_weights[layer], 2)
        return mix(blocks[layer], gating, gather(signal))

    gated = gated_of(current, peer, 0)
    (first,) = project(chan_scalar, gated, swap(gated, "chan"), out_weights[0], 1)
    first_home = across(first, 1, 0)

    gated = gated_of(first, swap(first, "chan"), 1)
    gated = jnp.where(section == 0, gated, across(gated, 1, 1))
    (second,) = project(chan_scalar, gated, swap(gated, "chan"), out_weights[1], 1)
    second_near = lax.ppermute(second, "section", [(0, 1)])

    mine = jnp.where(section == 0, first, second_near)
    other = jnp.where(section == 0, first_home, second)
    pair = jnp.where(sequence == 0, jnp.stack([mine, other]), jnp.stack([other, mine]))
    return pair[None]


def solution(mesh):
    placed = (
        P(None, "seq", "chan"),
        P("section", None, None, "chan"),
        P("section", "chan", None),
        P("section", None, "chan"),
        P(),
    )
    return jax.shard_map(
        per_device,
        mesh=mesh,
        in_specs=placed,
        out_specs=P("section", None, "seq", "chan"),
        check_vma=False,
    )
```

```python
import functools

import jax
import jax.numpy as jnp
from jax import lax
from jax.experimental import pallas as pl
from jax.experimental.pallas import tpu as pltpu
from jax.sharding import PartitionSpec as P


BAND = 8
REACH = BAND // 2
MB = 2


VMEM = pl.BlockSpec(memory_space=pltpu.VMEM)
SMEM = pl.BlockSpec(memory_space=pltpu.SMEM)


def call(kernel, outs, specs, flops, moved, grant=12, out_spec=VMEM):
    return pl.pallas_call(
        kernel,
        out_shape=outs,
        in_specs=specs,
        out_specs=jax.tree.map(lambda _: out_spec, outs),
        cost_estimate=pl.CostEstimate(flops=flops, bytes_accessed=moved, transcendentals=0),
        compiler_params=pltpu.CompilerParams(vmem_limit_bytes=grant << 20),
    )


def shape(*dims, dtype=jnp.bfloat16):
    return jax.ShapeDtypeStruct(dims, dtype)


def position():
    count = lax.axis_size("seq")
    place = lax.axis_index("seq")
    sequence = jnp.where(place >= count // 2, 1, 0)
    return sequence, lax.rem(place + lax.axis_index("section") * (count // 2), count)


def lag_of(slot, index):
    if lax.axis_size("seq") == BAND:
        return ((index - (index ^ slot) + REACH) & (BAND - 1)) - REACH
    return slot - REACH


def toeplitz_kernel(block, groups, layer, widths_ref, near_ref, far_ref, *refs):
    outs, flipped_ref = refs[:-1], refs[-1]
    heads, taps = near_ref.shape
    pieces = taps // block
    rows = lax.broadcasted_iota(jnp.int32, (block, block), 0)
    columns = lax.broadcasted_iota(jnp.int32, (block, block), 1)
    turn = (rows + columns == block - 1).astype(jnp.bfloat16)
    own = lax.axis_index("section") == layer
    sequence, index = position()
    width = widths_ref[sequence]
    for piece in range(pieces):
        at = slice(piece * block, (piece + 1) * block)
        taken = jnp.where(own, near_ref[:, at].astype(jnp.float32), far_ref[:, at].astype(jnp.float32))
        turned = jnp.dot(taken.astype(jnp.bfloat16), turn, preferred_element_type=jnp.float32)
        flipped_ref[:, taps - (piece + 1) * block : taps - piece * block] = turned
    for out_ref, slots in zip(outs, groups):
        for place, slot in enumerate(slots):
            lag = lag_of(slot, index)
            start = pl.multiple_of(block * (REACH - 1 - lag), block)
            window = flipped_ref[:, pl.ds(start, 2 * block)]
            band = (lag >= -width) & (lag < width)
            for head in range(heads):
                row = jnp.broadcast_to(window[head : head + 1, :], (block, 2 * block))
                turned = pltpu.roll(row, 1, 1, stride=1, stride_axis=0)[:, block:]
                kept = jnp.where(band, turned, 0.0)
                out_ref[head, :, place * block : (place + 1) * block] = kept.astype(jnp.bfloat16)


def toeplitz(layer, widths, near, far, block, groups):
    heads = near.shape[0]
    outs = tuple(shape(heads, block, len(slots) * block) for slots in groups)
    return pl.pallas_call(
        functools.partial(toeplitz_kernel, block, groups, layer),
        out_shape=outs,
        in_specs=[SMEM, VMEM, VMEM],
        out_specs=(VMEM,) * len(outs),
        scratch_shapes=[pltpu.VMEM(near.shape, jnp.float32)],
        name="toeplitz",
        cost_estimate=pl.CostEstimate(
            flops=heads * BAND * block * block * 40,
            bytes_accessed=heads * BAND * block * block * 2,
            transcendentals=0,
        ),
        compiler_params=pltpu.CompilerParams(vmem_limit_bytes=12 << 20),
    )(widths, near, far)


def mix_kernel(count, last, toeplitz_ref, *refs):
    sources, others, out_ref = refs[:count], refs[count:-1], refs[-1]
    heads = toeplitz_ref.shape[0]
    wide = out_ref.shape[1] // heads
    for head in range(heads):
        lanes = slice(head * wide, (head + 1) * wide)
        stacked = jnp.concatenate([source[:, lanes] for source in sources], axis=0)
        mixed = jnp.dot(toeplitz_ref[head], stacked, preferred_element_type=jnp.float32)
        if len(others) > last:
            mixed += others[-1][:, lanes]
        if last:
            gate = others[0][:, lanes].astype(jnp.float32)
            mixed = gate / (1.0 + jnp.exp(-gate)) * mixed
        out_ref[:, lanes] = mixed.astype(out_ref.dtype)


def mix(toeplitz_blocks, sources, total, gating):
    block, local = sources[0].shape
    last = gating is not None
    others = ([gating] if last else []) + ([total] if total is not None else [])
    return call(
        functools.partial(mix_kernel, len(sources), int(last)),
        shape(block, local, dtype=jnp.bfloat16 if last else jnp.float32),
        [VMEM] * (1 + len(sources) + len(others)),
        2 * len(sources) * block * block * local,
        toeplitz_blocks.size * 2 + (len(sources) + 4) * block * local * 2,
    )(toeplitz_blocks, *sources, *others)


def product(own_ref, peer_ref, weight_ref):
    depth = own_ref.shape[1]
    chan = lax.axis_index("chan")
    own_rows = weight_ref[pl.ds(pl.multiple_of(chan * depth, depth), depth), :]
    peer_rows = weight_ref[pl.ds(pl.multiple_of((1 - chan) * depth, depth), depth), :]
    total = jnp.dot(own_ref[...], own_rows, preferred_element_type=jnp.float32)
    return total + jnp.dot(peer_ref[...], peer_rows, preferred_element_type=jnp.float32)


def project_kernel(own_ref, peer_ref, weight_ref, *out_refs):
    total = product(own_ref, peer_ref, weight_ref)
    wide = total.shape[1] // len(out_refs)
    for at, out_ref in enumerate(out_refs):
        out_ref[...] = total[:, at * wide : (at + 1) * wide].astype(jnp.bfloat16)


def project(own, peer, weight, count):
    block, _ = own.shape
    return call(
        project_kernel,
        tuple(shape(block, weight.shape[1] // count) for _ in range(count)),
        [VMEM, VMEM, VMEM],
        2 * block * weight.size,
        2 * weight.size + 6 * own.size,
    )(own, peer, weight)


def step_kernel(own_ref, peer_ref, out_own_ref, out_peer_ref, *refs):
    in_ref, first_ref, signal_ref, gate_ref, all_ref = refs
    depth = own_ref.shape[1]
    chan = lax.axis_index("chan")
    at = pl.ds(pl.multiple_of(chan * depth, depth), depth)
    other = pl.ds(pl.multiple_of((1 - chan) * depth, depth), depth)
    all_ref[:, at] = own_ref[...]
    all_ref[:, other] = peer_ref[...]
    gated = all_ref[...]
    first = jnp.dot(gated, out_own_ref[...], preferred_element_type=jnp.float32).astype(jnp.bfloat16)
    second = jnp.dot(gated, out_peer_ref[...], preferred_element_type=jnp.float32).astype(jnp.bfloat16)
    first_ref[...] = first
    all_ref[:, at] = first
    all_ref[:, other] = second
    total = jnp.dot(all_ref[...], in_ref[...], preferred_element_type=jnp.float32)
    signal_ref[...] = total[:, :depth].astype(jnp.bfloat16)
    gate_ref[...] = total[:, depth:].astype(jnp.bfloat16)


def step(own, peer, out_own, out_peer, in_weight):
    block, depth = own.shape
    return pl.pallas_call(
        step_kernel,
        out_shape=(shape(block, depth),) * 3,
        in_specs=[VMEM] * 5,
        out_specs=(VMEM,) * 3,
        scratch_shapes=[pltpu.VMEM((block, 2 * depth), jnp.bfloat16)],
        name="step",
        cost_estimate=pl.CostEstimate(
            flops=16 * block * depth * depth, bytes_accessed=16 * depth * depth + 10 * own.size, transcendentals=0
        ),
        compiler_params=pltpu.CompilerParams(vmem_limit_bytes=12 << 20),
    )(own, peer, out_own, out_peer, in_weight)


def finish_kernel(own_ref, peer_ref, weight_ref, first_ref, first_home_ref, near_ref, out_ref):
    section = lax.axis_index("section")
    sequence, _ = position()

    @pl.when(section == 0)
    def _():
        out_ref[0, sequence] = first_ref[...]
        out_ref[0, 1 - sequence] = first_home_ref[...]

    @pl.when(section == 1)
    def _():
        out_ref[0, 1 - sequence] = product(own_ref, peer_ref, weight_ref).astype(jnp.bfloat16)
        out_ref[0, sequence] = near_ref[...]


def finish(own, peer, weight, first, first_home, near):
    block, local = first.shape
    return call(
        finish_kernel,
        shape(1, MB, block, local),
        [VMEM] * 6,
        4 * block * local * local,
        weight.size * 2 + 7 * own.size * 2,
        out_spec=pl.BlockSpec(),
    )(own, peer, weight, first, first_home, near)


def both_layers(tokens, in_proj, filters, out_proj, widths):
    count = lax.axis_size("seq")
    half = count // 2
    section = lax.axis_index("section")
    block = tokens.shape[1]
    sequence, _ = position()

    def swap(value, axis):
        return lax.ppermute(value, axis, [(0, 1), (1, 0)])

    def swap_in(value, at):
        return lax.ppermute(value, ("chan", "section"), [(at, 2 + at), (2 + at, at)])

    def across(value, from_section, to_section):
        pairs = [(2 * i + from_section, 2 * ((i + half) % count) + to_section) for i in range(count)]
        return lax.ppermute(value, ("seq", "section"), pairs)

    def pick(zero, one):
        return jnp.where(section == 0, zero, one)

    def where_held(which, held):
        low = held < half
        if which == 0:
            return (held, 0) if low else (held - half, 1)
        return (held + half, 1) if low else (held, 0)

    def ring(value, lag):
        pairs = []
        for which in range(MB):
            for held in range(count):
                source, target = where_held(which, held), where_held(which, (held + lag) % count)
                pairs.append((2 * source[0] + source[1], 2 * target[0] + target[1]))
        return lax.ppermute(value, ("seq", "section"), pairs)

    def halves(value):
        return value[: value.shape[0] // 2], value[value.shape[0] // 2 :]

    swapped = across(lax.dynamic_index_in_dim(tokens, 1 - sequence, 0, False), 1, 1)
    current = pick(lax.optimization_barrier(lax.dynamic_index_in_dim(tokens, sequence, 0, False)), swapped)
    peer = swap(current, "chan")

    in_near = in_proj[0].reshape(in_proj.shape[1], -1)
    in_far = swap(in_near, "section")
    taps = filters[0]
    far_taps = swap(taps, "section")
    out_near = out_proj[0]
    out_far = swap(out_near, "section")

    groups = ((0, REACH, 1, REACH + 1), (2, REACH + 2, REACH - 1, BAND - 1))
    blocks = []
    for layer in range(2):
        blocks.append(toeplitz(layer, widths, taps, far_taps, block, groups))

    def gathered(signal):
        if count != BAND:
            return [ring(signal, lag) if lag else signal for lag in range(-REACH, REACH)]
        near = [signal]
        for apart in range(1, REACH):
            near.append(lax.ppermute(signal, "seq", [(i, i ^ apart) for i in range(count)]))
        return near + [swap(value, "section") for value in near]

    def mixed(layer, sources, gating):
        total = None
        for group, members in enumerate(groups):
            last = group == len(groups) - 1
            chosen = [sources[slot] for slot in members]
            total = mix(blocks[layer][group], chosen, total, gating if last else None)
        return total

    in_first, in_last = pick(in_near, in_far), pick(in_far, in_near)
    signal, gating = project(current, peer, in_first, 2)
    sources = gathered(signal)

    upper, lower = halves(out_near)[0], halves(out_far)[1]
    sent, _ = lax.optimization_barrier((pick(upper, lower), signal))
    part = swap(sent, "chan")
    other = swap(part, "section")
    out_peer = pick(jnp.concatenate([part, other]), jnp.concatenate([other, part]))
    out_first, out_last = pick(out_near, out_far), pick(out_far, out_near)

    gated = mixed(0, sources, gating)
    gated_peer = swap(gated, "chan")
    first, signal, gating = step(gated, gated_peer, out_first, out_peer, in_last)
    gated = mixed(1, gathered(signal), gating)

    moved = across(gated, 1, 1)
    first_home = across(first, 1, 0)
    gated_peer = swap_in(gated, 0)
    (second,) = project(gated, gated_peer, out_last, 1)
    second_near = lax.ppermute(second, "section", [(0, 1)])
    moved_peer = swap_in(moved, 1)
    return finish(moved, moved_peer, out_last, first, first_home, second_near)


def solution(mesh):
    placed = (
        P(None, "seq", "chan"),
        P("section", None, None, "chan"),
        P("section", "chan", None),
        P("section", None, "chan"),
        P(),
    )
    return jax.shard_map(
        both_layers,
        mesh=mesh,
        in_specs=placed,
        out_specs=P("section", None, "seq", "chan"),
        check_vma=False,
    )
```

```python
import functools

import jax
import jax.numpy as jnp
from jax import lax
from jax.experimental import pallas as pl
from jax.experimental.pallas import tpu as pltpu
from jax.sharding import PartitionSpec as P


BAND = 8
REACH = BAND // 2
MB = 2
PARTS = 2


VMEM = pl.BlockSpec(memory_space=pltpu.VMEM)
SMEM = pl.BlockSpec(memory_space=pltpu.SMEM)


def call(kernel, outs, specs, flops, moved, grant=12, out_spec=VMEM):
    return pl.pallas_call(
        kernel,
        out_shape=outs,
        in_specs=specs,
        out_specs=jax.tree.map(lambda _: out_spec, outs),
        cost_estimate=pl.CostEstimate(flops=flops, bytes_accessed=moved, transcendentals=0),
        compiler_params=pltpu.CompilerParams(vmem_limit_bytes=grant << 20),
    )


def shape(*dims, dtype=jnp.bfloat16):
    return jax.ShapeDtypeStruct(dims, dtype)


def position():
    count = lax.axis_size("seq")
    place = lax.axis_index("seq")
    sequence = jnp.where(place >= count // 2, 1, 0)
    return sequence, lax.rem(place + lax.axis_index("section") * (count // 2), count)


def lag_of(slot, index):
    if lax.axis_size("seq") == BAND:
        return ((index - (index ^ slot) + REACH) & (BAND - 1)) - REACH
    return slot - REACH


def toeplitz_kernel(block, groups, layer, widths_ref, near_ref, far_ref, *refs):
    outs, flipped_ref = refs[:-1], refs[-1]
    heads, taps = near_ref.shape
    pieces = taps // block
    rows = lax.broadcasted_iota(jnp.int32, (block, block), 0)
    columns = lax.broadcasted_iota(jnp.int32, (block, block), 1)
    turn = (rows + columns == block - 1).astype(jnp.bfloat16)
    own = lax.axis_index("section") == layer
    sequence, index = position()
    width = widths_ref[sequence]
    for piece in range(pieces):
        at = slice(piece * block, (piece + 1) * block)
        taken = jnp.where(own, near_ref[:, at].astype(jnp.float32), far_ref[:, at].astype(jnp.float32))
        turned = jnp.dot(taken.astype(jnp.bfloat16), turn, preferred_element_type=jnp.float32)
        flipped_ref[:, taps - (piece + 1) * block : taps - piece * block] = turned
    for out_ref, slots in zip(outs, groups):
        for place, slot in enumerate(slots):
            lag = lag_of(slot, index)
            start = pl.multiple_of(block * (REACH - 1 - lag), block)
            window = flipped_ref[:, pl.ds(start, 2 * block)]
            band = (lag >= -width) & (lag < width)
            for head in range(heads):
                row = jnp.broadcast_to(window[head : head + 1, :], (block, 2 * block))
                turned = pltpu.roll(row, 1, 1, stride=1, stride_axis=0)[:, block:]
                kept = jnp.where(band, turned, 0.0)
                out_ref[head, :, place * block : (place + 1) * block] = kept.astype(jnp.bfloat16)


def toeplitz(layer, widths, near, far, block, groups):
    heads = near.shape[0]
    outs = tuple(shape(heads, block, len(slots) * block) for slots in groups)
    return pl.pallas_call(
        functools.partial(toeplitz_kernel, block, groups, layer),
        out_shape=outs,
        in_specs=[SMEM, VMEM, VMEM],
        out_specs=(VMEM,) * len(outs),
        scratch_shapes=[pltpu.VMEM(near.shape, jnp.float32)],
        name="toeplitz",
        cost_estimate=pl.CostEstimate(
            flops=heads * BAND * block * block * 40,
            bytes_accessed=heads * BAND * block * block * 2,
            transcendentals=0,
        ),
        compiler_params=pltpu.CompilerParams(vmem_limit_bytes=12 << 20),
    )(widths, near, far)


def take_kernel(tokens_ref, *refs):
    outs, sems = refs[:-1], refs[-1]
    sequence, _ = position()
    parts = len(outs) // 2
    rows = outs[0].shape[0]
    copies = []
    for at, out_ref in enumerate(outs):
        held = 1 - sequence if at < parts else sequence
        source = tokens_ref.at[held, pl.ds((at % parts) * rows, rows), :]
        copies.append(pltpu.make_async_copy(source, out_ref, sems.at[at]))
        copies[-1].start()
    for copy in copies:
        copy.wait()


def take(tokens, parts):
    _, block, local = tokens.shape
    outs = pl.pallas_call(
        take_kernel,
        out_shape=(shape(block // parts, local),) * (2 * parts),
        in_specs=[pl.BlockSpec(memory_space=pl.ANY)],
        out_specs=(VMEM,) * (2 * parts),
        scratch_shapes=[pltpu.SemaphoreType.DMA((2 * parts,))],
        name="take",
        cost_estimate=pl.CostEstimate(flops=0, bytes_accessed=4 * tokens.size, transcendentals=0),
        compiler_params=pltpu.CompilerParams(vmem_limit_bytes=4 << 20),
    )(tokens)
    return outs[:parts], outs[parts:]


def mix_kernel(count, last, toeplitz_ref, *refs):
    sources, refs = refs[:count], refs[count:]
    gate_ref, refs = (refs[0], refs[1:]) if last else (None, refs)
    total_ref, outs = refs[0] if last else None, refs[1:] if last else refs
    heads = toeplitz_ref.shape[0]
    wide = outs[0].shape[1] // heads
    for head in range(heads):
        lanes = slice(head * wide, (head + 1) * wide)
        stacked = jnp.concatenate([source[:, lanes] for source in sources], axis=0)
        mixed = jnp.dot(toeplitz_ref[head], stacked, preferred_element_type=jnp.float32)
        if last:
            mixed += total_ref[:, lanes]
            gate = gate_ref[:, lanes].astype(jnp.float32)
            mixed = gate / (1.0 + jnp.exp(-gate)) * mixed
        mixed = mixed.astype(outs[0].dtype)
        outs[0][:, lanes] = mixed
        for at, out_ref in enumerate(outs[1:]):
            rows = out_ref.shape[0]
            out_ref[:, lanes] = mixed[at * rows : (at + 1) * rows]


def mix(toeplitz_blocks, sources, total, gating, parts):
    block, local = sources[0].shape
    last = gating is not None
    others = [gating, total] if last else []
    outs = (shape(block, local, dtype=jnp.bfloat16 if last else jnp.float32),)
    if parts > 1:
        outs += (shape(block // parts, local),) * parts
    return call(
        functools.partial(mix_kernel, len(sources), last),
        outs,
        [VMEM] * (1 + len(sources) + len(others)),
        2 * len(sources) * block * block * local,
        toeplitz_blocks.size * 2 + (len(sources) + 4) * block * local * 2,
    )(toeplitz_blocks, *sources, *others)


def rows_of(refs):
    return refs[0][...] if len(refs) == 1 else jnp.concatenate([ref[...] for ref in refs], axis=0)


def product(own_refs, peer_refs, weight_ref):
    depth = own_refs[0].shape[1]
    chan = lax.axis_index("chan")
    own_rows = weight_ref[pl.ds(pl.multiple_of(chan * depth, depth), depth), :]
    peer_rows = weight_ref[pl.ds(pl.multiple_of((1 - chan) * depth, depth), depth), :]
    total = jnp.dot(rows_of(own_refs), own_rows, preferred_element_type=jnp.float32)
    return total + jnp.dot(rows_of(peer_refs), peer_rows, preferred_element_type=jnp.float32)


def project_kernel(parts, weight_ref, *refs):
    own_refs, peer_refs, out_refs = refs[:parts], refs[parts : 2 * parts], refs[2 * parts :]
    total = product(own_refs, peer_refs, weight_ref)
    wide = total.shape[1] // len(out_refs)
    for at, out_ref in enumerate(out_refs):
        out_ref[...] = total[:, at * wide : (at + 1) * wide].astype(jnp.bfloat16)


def project(own, peer, weight, count):
    block = own[0].shape[0] * len(own)
    return call(
        functools.partial(project_kernel, len(own)),
        tuple(shape(block, weight.shape[1] // count) for _ in range(count)),
        [VMEM] * (1 + 2 * len(own)),
        2 * block * weight.size,
        2 * weight.size + 4 * block * weight.shape[0],
    )(weight, *own, *peer)


def step_kernel(own_ref, peer_ref, out_own_ref, out_peer_ref, *refs):
    in_ref, first_ref, signal_ref, gate_ref, all_ref = refs
    depth = own_ref.shape[1]
    chan = lax.axis_index("chan")
    at = pl.ds(pl.multiple_of(chan * depth, depth), depth)
    other = pl.ds(pl.multiple_of((1 - chan) * depth, depth), depth)
    all_ref[:, at] = own_ref[...]
    all_ref[:, other] = peer_ref[...]
    gated = all_ref[...]
    first = jnp.dot(gated, out_own_ref[...], preferred_element_type=jnp.float32).astype(jnp.bfloat16)
    second = jnp.dot(gated, out_peer_ref[...], preferred_element_type=jnp.float32).astype(jnp.bfloat16)
    first_ref[...] = first
    all_ref[:, at] = first
    all_ref[:, other] = second
    total = jnp.dot(all_ref[...], in_ref[...], preferred_element_type=jnp.float32)
    signal_ref[...] = total[:, :depth].astype(jnp.bfloat16)
    gate_ref[...] = total[:, depth:].astype(jnp.bfloat16)


def step(own, peer, out_own, out_peer, in_weight):
    block, depth = own.shape
    return pl.pallas_call(
        step_kernel,
        out_shape=(shape(block, depth),) * 3,
        in_specs=[VMEM] * 5,
        out_specs=(VMEM,) * 3,
        scratch_shapes=[pltpu.VMEM((block, 2 * depth), jnp.bfloat16)],
        name="step",
        cost_estimate=pl.CostEstimate(
            flops=16 * block * depth * depth, bytes_accessed=16 * depth * depth + 10 * own.size, transcendentals=0
        ),
        compiler_params=pltpu.CompilerParams(vmem_limit_bytes=12 << 20),
    )(own, peer, out_own, out_peer, in_weight)


def finish_kernel(parts, weight_ref, first_ref, first_home_ref, near_ref, *refs):
    own_refs, peer_refs, out_ref = refs[:parts], refs[parts:-1], refs[-1]
    section = lax.axis_index("section")
    sequence, _ = position()

    @pl.when(section == 0)
    def _():
        out_ref[0, sequence] = first_ref[...]
        out_ref[0, 1 - sequence] = first_home_ref[...]

    @pl.when(section == 1)
    def _():
        out_ref[0, 1 - sequence] = product(own_refs, peer_refs, weight_ref).astype(jnp.bfloat16)
        out_ref[0, sequence] = near_ref[...]


def finish(own, peer, weight, first, first_home, near):
    block, local = first.shape
    return call(
        functools.partial(finish_kernel, len(own)),
        shape(1, MB, block, local),
        [VMEM] * (4 + 2 * len(own)),
        2 * block * weight.size,
        weight.size * 2 + 14 * first.size,
        out_spec=pl.BlockSpec(),
    )(weight, first, first_home, near, *own, *peer)


def both_layers(tokens, in_proj, filters, out_proj, widths):
    count = lax.axis_size("seq")
    half = count // 2
    section = lax.axis_index("section")
    block = tokens.shape[1]
    _, _ = position()

    def swap(value, axis):
        return lax.ppermute(value, axis, [(0, 1), (1, 0)])

    def swap_in(value, at):
        return lax.ppermute(value, ("chan", "section"), [(at, 2 + at), (2 + at, at)])

    def across(value, from_section, to_section):
        pairs = [(2 * i + from_section, 2 * ((i + half) % count) + to_section) for i in range(count)]
        return lax.ppermute(value, ("seq", "section"), pairs)

    def pick(zero, one):
        return jnp.where(section == 0, zero, one)

    def where_held(which, held):
        low = held < half
        if which == 0:
            return (held, 0) if low else (held - half, 1)
        return (held + half, 1) if low else (held, 0)

    def ring(value, lag):
        pairs = []
        for which in range(MB):
            for held in range(count):
                source, target = where_held(which, held), where_held(which, (held + lag) % count)
                pairs.append((2 * source[0] + source[1], 2 * target[0] + target[1]))
        return lax.ppermute(value, ("seq", "section"), pairs)

    def halves(value):
        return value[: value.shape[0] // 2], value[value.shape[0] // 2 :]

    def each(move, values):
        moved = []
        for value in values:
            moved.append(move(value))
        return moved

    other_tokens, own_tokens = take(tokens, PARTS)
    swapped = each(lambda value: across(value, 1, 1), other_tokens)
    current = [pick(own, moved) for own, moved in zip(own_tokens, swapped)]
    peer = each(lambda value: swap(value, "chan"), current)

    in_near = in_proj[0].reshape(in_proj.shape[1], -1)
    in_far = swap(in_near, "section")
    taps = filters[0]
    far_taps = swap(taps, "section")
    out_near = out_proj[0]
    out_far = swap(out_near, "section")

    groups = ((0, REACH, 1, REACH + 1), (2, REACH + 2, REACH - 1, BAND - 1))
    blocks = []
    for layer in range(2):
        blocks.append(toeplitz(layer, widths, taps, far_taps, block, groups))

    def gathered(signal):
        if count != BAND:
            return [ring(signal, lag) if lag else signal for lag in range(-REACH, REACH)]
        near = [signal]
        for apart in range(1, REACH):
            near.append(lax.ppermute(signal, "seq", [(i, i ^ apart) for i in range(count)]))
        return near + each(lambda value: swap(value, "section"), near)

    def mixed(layer, sources, gating, parts):
        total = (None,)
        for group, members in enumerate(groups):
            last = group == len(groups) - 1
            chosen = [sources[slot] for slot in members]
            total = mix(blocks[layer][group], chosen, total[0], gating if last else None, parts if last else 1)
        return total

    in_first, in_last = pick(in_near, in_far), pick(in_far, in_near)
    signal, gating = project(current, peer, in_first, 2)
    sources = gathered(signal)

    upper, lower = halves(out_near)[0], halves(out_far)[1]
    sent, _ = lax.optimization_barrier((pick(upper, lower), signal))
    part = swap(sent, "chan")
    other = swap(part, "section")
    out_peer = pick(jnp.concatenate([part, other]), jnp.concatenate([other, part]))
    out_first, out_last = pick(out_near, out_far), pick(out_far, out_near)

    (gated,) = mixed(0, sources, gating, 1)
    gated_peer = swap(gated, "chan")
    first, signal, gating = step(gated, gated_peer, out_first, out_peer, in_last)
    sources = gathered(signal)
    first_home = across(first, 1, 0)
    gated, *parts = mixed(1, sources, gating, PARTS)

    moved = each(lambda value: across(value, 1, 1), parts)
    gated_peer = swap_in(gated, 0)
    (second,) = project([gated], [gated_peer], out_last, 1)
    second_near = lax.ppermute(second, "section", [(0, 1)])
    moved_peer = each(lambda value: swap_in(value, 1), moved)
    return finish(moved, moved_peer, out_last, first, first_home, second_near)


def solution(mesh):
    placed = (
        P(None, "seq", "chan"),
        P("section", None, None, "chan"),
        P("section", "chan", None),
        P("section", None, "chan"),
        P(),
    )
    return jax.shard_map(
        both_layers,
        mesh=mesh,
        in_specs=placed,
        out_specs=P("section", None, "seq", "chan"),
        check_vma=False,
    )
```

```python
import functools

import jax
import jax.numpy as jnp
from jax import lax
from jax.experimental import pallas as pl
from jax.experimental.pallas import tpu as pltpu
from jax.sharding import PartitionSpec as P


BAND = 8
REACH = BAND // 2
MB = 2
LEAVING, HOMING = 1, 1 / 2
GROUPS = ((0, REACH, 1, REACH + 1, 2, REACH + 2), (3, REACH + 3))


VMEM = pl.BlockSpec(memory_space=pltpu.VMEM)
SMEM = pl.BlockSpec(memory_space=pltpu.SMEM)


def call(kernel, outs, specs, flops, moved, grant=12, out_spec=VMEM):
    return pl.pallas_call(
        kernel,
        out_shape=outs,
        in_specs=specs,
        out_specs=jax.tree.map(lambda _: out_spec, outs),
        cost_estimate=pl.CostEstimate(flops=flops, bytes_accessed=moved, transcendentals=0),
        compiler_params=pltpu.CompilerParams(vmem_limit_bytes=grant << 20),
    )


def shape(*dims, dtype=jnp.bfloat16):
    return jax.ShapeDtypeStruct(dims, dtype)


def two_parts(block, share):
    first = round(block * share / 16) * 16
    return tuple(rows for rows in (first, block - first) if rows)


def position():
    count = lax.axis_size("seq")
    place = lax.axis_index("seq")
    sequence = jnp.where(place >= count // 2, 1, 0)
    return sequence, lax.rem(place + lax.axis_index("section") * (count // 2), count)


def lag_of(slot, index):
    if lax.axis_size("seq") == BAND:
        return ((index - (index ^ slot) + REACH) & (BAND - 1)) - REACH
    return slot - REACH


def toeplitz_kernel(block, groups, layer, widths_ref, near_ref, far_ref, *refs):
    outs, flipped_ref = refs[:-1], refs[-1]
    heads, taps = near_ref.shape
    pieces = taps // block
    rows = lax.broadcasted_iota(jnp.int32, (block, block), 0)
    columns = lax.broadcasted_iota(jnp.int32, (block, block), 1)
    turn = (rows + columns == block - 1).astype(jnp.bfloat16)
    own = lax.axis_index("section") == layer
    sequence, index = position()
    width = widths_ref[sequence]
    for piece in range(pieces):
        at = slice(piece * block, (piece + 1) * block)
        taken = jnp.where(own, near_ref[:, at].astype(jnp.float32), far_ref[:, at].astype(jnp.float32))
        turned = jnp.dot(taken.astype(jnp.bfloat16), turn, preferred_element_type=jnp.float32)
        flipped_ref[:, taps - (piece + 1) * block : taps - piece * block] = turned
    for out_ref, slots in zip(outs, groups):
        for place, slot in enumerate(slots):
            lag = lag_of(slot, index)
            start = pl.multiple_of(block * (REACH - 1 - lag), block)
            window = flipped_ref[:, pl.ds(start, 2 * block)]
            band = (lag >= -width) & (lag < width)
            for head in range(heads):
                row = jnp.broadcast_to(window[head : head + 1, :], (block, 2 * block))
                turned = pltpu.roll(row, 1, 1, stride=1, stride_axis=0)[:, block:]
                kept = jnp.where(band, turned, 0.0)
                out_ref[head, :, place * block : (place + 1) * block] = kept.astype(jnp.bfloat16)


def toeplitz(layer, widths, near, far, block, groups):
    heads = near.shape[0]
    outs = tuple(shape(heads, block, len(slots) * block) for slots in groups)
    return pl.pallas_call(
        functools.partial(toeplitz_kernel, block, groups, layer),
        out_shape=outs,
        in_specs=[SMEM, VMEM, VMEM],
        out_specs=(VMEM,) * len(outs),
        scratch_shapes=[pltpu.VMEM(near.shape, jnp.float32)],
        name="toeplitz",
        cost_estimate=pl.CostEstimate(
            flops=heads * BAND * block * block * 40,
            bytes_accessed=heads * BAND * block * block * 2,
            transcendentals=0,
        ),
        compiler_params=pltpu.CompilerParams(vmem_limit_bytes=12 << 20),
    )(widths, near, far)


def take_kernel(tokens_ref, *refs):
    outs, sems = refs[:-1], refs[-1]
    sequence, _ = position()
    copies, start = [], 0
    for at, out_ref in enumerate(outs):
        held = 1 - sequence if at < len(outs) // 2 else sequence
        rows = out_ref.shape[0]
        source = tokens_ref.at[held, pl.ds(start, rows), :]
        start = (start + rows) % tokens_ref.shape[1]
        copies.append(pltpu.make_async_copy(source, out_ref, sems.at[at]))
        copies[-1].start()
    for copy in copies:
        copy.wait()


def take(tokens, parts):
    local = tokens.shape[2]
    outs = pl.pallas_call(
        take_kernel,
        out_shape=tuple(shape(rows, local) for rows in parts) * 2,
        in_specs=[pl.BlockSpec(memory_space=pltpu.HBM)],
        out_specs=(VMEM,) * (2 * len(parts)),
        scratch_shapes=[pltpu.SemaphoreType.DMA((2 * len(parts),))],
        name="take",
        cost_estimate=pl.CostEstimate(flops=0, bytes_accessed=4 * tokens.size, transcendentals=0),
        compiler_params=pltpu.CompilerParams(vmem_limit_bytes=4 << 20),
    )(pltpu.with_memory_space_constraint(tokens, pltpu.HBM))
    return outs[: len(parts)], outs[len(parts) :]


def mix_kernel(count, last, toeplitz_ref, *refs):
    sources, refs = refs[:count], refs[count:]
    gate_ref, refs = (refs[0], refs[1:]) if last else (None, refs)
    total_ref, outs = refs[0] if last else None, refs[1:] if last else refs
    heads = toeplitz_ref.shape[0]
    wide = outs[0].shape[1] // heads
    for head in range(heads):
        lanes = slice(head * wide, (head + 1) * wide)
        stacked = jnp.concatenate([source[:, lanes] for source in sources], axis=0)
        mixed = jnp.dot(toeplitz_ref[head], stacked, preferred_element_type=jnp.float32)
        if last:
            mixed += total_ref[:, lanes]
            gate = gate_ref[:, lanes].astype(jnp.float32)
            mixed = gate / (1.0 + jnp.exp(-gate)) * mixed
        mixed = mixed.astype(outs[0].dtype)
        outs[0][:, lanes] = mixed
        start = 0
        for out_ref in outs[1:]:
            out_ref[:, lanes] = mixed[start : start + out_ref.shape[0]]
            start += out_ref.shape[0]


def mix(toeplitz_blocks, sources, total, gating, parts):
    block, local = sources[0].shape
    last = gating is not None
    others = [gating, total] if last else []
    outs = (shape(block, local, dtype=jnp.bfloat16 if last else jnp.float32),)
    outs += tuple(shape(rows, local) for rows in parts)
    return call(
        functools.partial(mix_kernel, len(sources), last),
        outs,
        [VMEM] * (1 + len(sources) + len(others)),
        2 * len(sources) * block * block * local,
        toeplitz_blocks.size * 2 + (len(sources) + 4) * block * local * 2,
    )(toeplitz_blocks, *sources, *others)


def rows_of(refs):
    return refs[0][...] if len(refs) == 1 else jnp.concatenate([ref[...] for ref in refs], axis=0)


def product(own_refs, peer_refs, weight_ref):
    depth = own_refs[0].shape[1]
    chan = lax.axis_index("chan")
    own_rows = weight_ref[pl.ds(pl.multiple_of(chan * depth, depth), depth), :]
    peer_rows = weight_ref[pl.ds(pl.multiple_of((1 - chan) * depth, depth), depth), :]
    total = jnp.dot(rows_of(own_refs), own_rows, preferred_element_type=jnp.float32)
    return total + jnp.dot(rows_of(peer_refs), peer_rows, preferred_element_type=jnp.float32)


def project_kernel(parts, weight_ref, *refs):
    own_refs, peer_refs, out_refs = refs[:parts], refs[parts : 2 * parts], refs[2 * parts :]
    total = product(own_refs, peer_refs, weight_ref)
    wide = total.shape[1] // len(out_refs)
    for at, out_ref in enumerate(out_refs):
        out_ref[...] = total[:, at * wide : (at + 1) * wide].astype(jnp.bfloat16)


def project(own, peer, weight, count):
    block = sum(value.shape[0] for value in own)
    return call(
        functools.partial(project_kernel, len(own)),
        tuple(shape(block, weight.shape[1] // count) for _ in range(count)),
        [VMEM] * (1 + 2 * len(own)),
        2 * block * weight.size,
        2 * weight.size + 4 * block * weight.shape[0],
    )(weight, *own, *peer)


def step_kernel(own_ref, peer_ref, out_own_ref, out_peer_ref, *refs):
    in_ref, first_ref, signal_ref, gate_ref, all_ref = refs
    depth = own_ref.shape[1]
    chan = lax.axis_index("chan")
    at = pl.ds(pl.multiple_of(chan * depth, depth), depth)
    other = pl.ds(pl.multiple_of((1 - chan) * depth, depth), depth)
    all_ref[:, at] = own_ref[...]
    all_ref[:, other] = peer_ref[...]
    gated = all_ref[...]
    first = jnp.dot(gated, out_own_ref[...], preferred_element_type=jnp.float32).astype(jnp.bfloat16)
    second = jnp.dot(gated, out_peer_ref[...], preferred_element_type=jnp.float32).astype(jnp.bfloat16)
    first_ref[...] = first
    all_ref[:, at] = first
    all_ref[:, other] = second
    total = jnp.dot(all_ref[...], in_ref[...], preferred_element_type=jnp.float32)
    signal_ref[...] = total[:, :depth].astype(jnp.bfloat16)
    gate_ref[...] = total[:, depth:].astype(jnp.bfloat16)


def step(own, peer, out_own, out_peer, in_weight):
    block, depth = own.shape
    return pl.pallas_call(
        step_kernel,
        out_shape=(shape(block, depth),) * 3,
        in_specs=[VMEM] * 5,
        out_specs=(VMEM,) * 3,
        scratch_shapes=[pltpu.VMEM((block, 2 * depth), jnp.bfloat16)],
        name="step",
        cost_estimate=pl.CostEstimate(
            flops=16 * block * depth * depth, bytes_accessed=16 * depth * depth + 10 * own.size, transcendentals=0
        ),
        compiler_params=pltpu.CompilerParams(vmem_limit_bytes=12 << 20),
    )(own, peer, out_own, out_peer, in_weight)


def finish_kernel(weight_ref, first_ref, first_home_ref, near_ref, home_ref, own_ref, peer_ref, out_ref):
    section = lax.axis_index("section")
    sequence, _ = position()
    rows = home_ref.shape[0]

    @pl.when(section == 0)
    def _():
        out_ref[0, sequence] = first_ref[...]
        out_ref[0, 1 - sequence] = first_home_ref[...]

    @pl.when(section == 1)
    def _():
        out_ref[0, 1 - sequence, :rows] = home_ref[...]
        out_ref[0, 1 - sequence, rows:] = product([own_ref], [peer_ref], weight_ref).astype(jnp.bfloat16)
        out_ref[0, sequence] = near_ref[...]


def finish(weight, first, first_home, near, home, own, peer):
    block, local = first.shape
    return call(
        finish_kernel,
        shape(1, MB, block, local),
        [VMEM] * 7,
        block * weight.size,
        weight.size * 2 + 12 * first.size,
        out_spec=pl.BlockSpec(),
    )(weight, first, first_home, near, home, own, peer)


def both_layers(tokens, in_proj, filters, out_proj, widths):
    count = lax.axis_size("seq")
    half = count // 2
    section = lax.axis_index("section")
    block = tokens.shape[1]
    _, _ = position()

    def swap(value, axis):
        return lax.ppermute(value, axis, [(0, 1), (1, 0)])

    def across(value, from_section, to_section):
        pairs = [(2 * i + from_section, 2 * ((i + half) % count) + to_section) for i in range(count)]
        return lax.ppermute(value, ("seq", "section"), pairs)

    def pick(zero, one):
        return jnp.where(section == 0, zero, one)

    def where_held(which, held):
        low = held < half
        if which == 0:
            return (held, 0) if low else (held - half, 1)
        return (held + half, 1) if low else (held, 0)

    def ring(value, lag):
        pairs = []
        for which in range(MB):
            for held in range(count):
                source, target = where_held(which, held), where_held(which, (held + lag) % count)
                pairs.append((2 * source[0] + source[1], 2 * target[0] + target[1]))
        return lax.ppermute(value, ("seq", "section"), pairs)

    def halves(value):
        return value[: value.shape[0] // 2], value[value.shape[0] // 2 :]

    def each(move, values):
        moved = []
        for value in values:
            moved.append(move(value))
        return moved

    other_tokens, own_tokens = take(tokens, two_parts(block, LEAVING))
    swapped = each(lambda value: across(value, 1, 1), other_tokens)
    current = [pick(own, moved) for own, moved in zip(own_tokens, swapped)]
    peer = each(lambda value: swap(value, "chan"), current)

    in_near = in_proj[0].reshape(in_proj.shape[1], -1)
    in_far = swap(in_near, "section")
    taps = filters[0]
    far_taps = swap(taps, "section")
    out_near = out_proj[0]
    out_far = swap(out_near, "section")

    groups = GROUPS
    blocks = []
    for layer in range(2):
        blocks.append(toeplitz(layer, widths, taps, far_taps, block, groups))

    def gathered(signal):
        if count != BAND:
            return [ring(signal, lag) if lag else signal for lag in range(-REACH, REACH)]
        near = [signal]
        for apart in range(1, REACH):
            near.append(lax.ppermute(signal, "seq", [(i, i ^ apart) for i in range(count)]))
        return near + each(lambda value: swap(value, "section"), near)

    def mixed(layer, sources, gating, parts):
        total = (None,)
        for group, members in enumerate(groups):
            last = group == len(groups) - 1
            chosen = [sources[slot] for slot in members]
            total = mix(blocks[layer][group], chosen, total[0], gating if last else None, parts if last else ())
        return total

    in_first, in_last = pick(in_near, in_far), pick(in_far, in_near)
    signal, gating = project(current, peer, in_first, 2)
    sources = gathered(signal)

    upper, lower = halves(out_near)[0], halves(out_far)[1]
    sent, _ = lax.optimization_barrier((pick(upper, lower), signal))
    part = swap(sent, "chan")
    other = swap(part, "section")
    out_peer = pick(jnp.concatenate([part, other]), jnp.concatenate([other, part]))
    out_first, out_last = pick(out_near, out_far), pick(out_far, out_near)

    (gated,) = mixed(0, sources, gating, ())
    gated_peer = swap(gated, "chan")
    gated_home = across(gated, 1, 0)
    first, signal, gating = step(gated, gated_peer, out_first, out_peer, in_last)
    sources = gathered(signal)
    home_peer = swap(gated_home, "chan")
    (first_home,) = project([gated_home], [home_peer], out_first, 1)
    gated, upper, lower = mixed(1, sources, gating, two_parts(block, HOMING))

    upper_peer = swap(upper, "chan")
    lower_home = across(lower, 1, 1)
    near_peer = lax.ppermute(gated, ("chan", "section"), [(0, 3), (2, 1)])
    near_own = lax.ppermute(gated, "section", [(0, 1)])
    (second_upper,) = project([upper], [upper_peer], out_last, 1)
    upper_home = across(second_upper, 1, 1)
    (second_near,) = project([near_own], [near_peer], out_last, 1)
    lower_home_peer = swap(lower_home, "chan")
    return finish(out_last, first, first_home, second_near, upper_home, lower_home, lower_home_peer)


def solution(mesh):
    placed = (
        P(None, "seq", "chan"),
        P("section", None, None, "chan"),
        P("section", "chan", None),
        P("section", None, "chan"),
        P(),
    )
    return jax.shard_map(
        both_layers,
        mesh=mesh,
        in_specs=placed,
        out_specs=P("section", None, "seq", "chan"),
        check_vma=False,
    )
```

```python
import functools

import jax
import jax.numpy as jnp
from jax import lax
from jax.experimental import pallas as pl
from jax.experimental.pallas import tpu as pltpu
from jax.sharding import PartitionSpec as P


BAND = 8
REACH = BAND // 2
MB = 2
LEAVING, HOMING = 1, 1 / 2
GROUPS = ((0, REACH, 1, REACH + 1, 2, REACH + 2), (3, REACH + 3))


VMEM = pl.BlockSpec(memory_space=pltpu.VMEM)
SMEM = pl.BlockSpec(memory_space=pltpu.SMEM)


def call(kernel, outs, specs, flops, moved, grant=12, out_spec=VMEM):
    return pl.pallas_call(
        kernel,
        out_shape=outs,
        in_specs=specs,
        out_specs=jax.tree.map(lambda _: out_spec, outs),
        cost_estimate=pl.CostEstimate(flops=flops, bytes_accessed=moved, transcendentals=0),
        compiler_params=pltpu.CompilerParams(vmem_limit_bytes=grant << 20),
    )


def shape(*dims, dtype=jnp.bfloat16):
    return jax.ShapeDtypeStruct(dims, dtype)


def two_parts(block, share):
    first = round(block * share / 16) * 16
    return tuple(rows for rows in (first, block - first) if rows)


def position():
    count = lax.axis_size("seq")
    place = lax.axis_index("seq")
    sequence = jnp.where(place >= count // 2, 1, 0)
    return sequence, lax.rem(place + lax.axis_index("section") * (count // 2), count)


def lag_of(slot, index):
    if lax.axis_size("seq") == BAND:
        return ((index - (index ^ slot) + REACH) & (BAND - 1)) - REACH
    return slot - REACH


def toeplitz_kernel(block, groups, layer, widths_ref, near_ref, far_ref, *refs):
    outs, flipped_ref = refs[:-1], refs[-1]
    heads, taps = near_ref.shape
    pieces = taps // block
    rows = lax.broadcasted_iota(jnp.int32, (block, block), 0)
    columns = lax.broadcasted_iota(jnp.int32, (block, block), 1)
    turn = (rows + columns == block - 1).astype(jnp.bfloat16)
    own = lax.axis_index("section") == layer
    sequence, index = position()
    width = widths_ref[sequence]
    for piece in range(pieces):
        at = slice(piece * block, (piece + 1) * block)
        taken = jnp.where(own, near_ref[:, at].astype(jnp.float32), far_ref[:, at].astype(jnp.float32))
        turned = jnp.dot(taken.astype(jnp.bfloat16), turn, preferred_element_type=jnp.float32)
        flipped_ref[:, taps - (piece + 1) * block : taps - piece * block] = turned
    for out_ref, slots in zip(outs, groups):
        for place, slot in enumerate(slots):
            lag = lag_of(slot, index)
            start = pl.multiple_of(block * (REACH - 1 - lag), block)
            window = flipped_ref[:, pl.ds(start, 2 * block)]
            band = (lag >= -width) & (lag < width)
            for head in range(heads):
                row = jnp.broadcast_to(window[head : head + 1, :], (block, 2 * block))
                turned = pltpu.roll(row, 1, 1, stride=1, stride_axis=0)[:, block:]
                kept = jnp.where(band, turned, 0.0)
                out_ref[head, :, place * block : (place + 1) * block] = kept.astype(jnp.bfloat16)


def toeplitz(layer, widths, near, far, block, groups):
    heads = near.shape[0]
    outs = tuple(shape(heads, block, len(slots) * block) for slots in groups)
    return pl.pallas_call(
        functools.partial(toeplitz_kernel, block, groups, layer),
        out_shape=outs,
        in_specs=[SMEM, VMEM, VMEM],
        out_specs=(VMEM,) * len(outs),
        scratch_shapes=[pltpu.VMEM(near.shape, jnp.float32)],
        name="toeplitz",
        cost_estimate=pl.CostEstimate(
            flops=heads * BAND * block * block * 40,
            bytes_accessed=heads * BAND * block * block * 2,
            transcendentals=0,
        ),
        compiler_params=pltpu.CompilerParams(vmem_limit_bytes=12 << 20),
    )(widths, near, far)


def take_kernel(tokens_ref, *refs):
    outs, sems = refs[:-1], refs[-1]
    sequence, _ = position()
    copies, start = [], 0
    for at, out_ref in enumerate(outs):
        held = 1 - sequence if at < len(outs) // 2 else sequence
        rows = out_ref.shape[0]
        source = tokens_ref.at[held, pl.ds(start, rows), :]
        start = (start + rows) % tokens_ref.shape[1]
        copies.append(pltpu.make_async_copy(source, out_ref, sems.at[at]))
        copies[-1].start()
    for copy in copies:
        copy.wait()


def take(tokens, parts):
    local = tokens.shape[2]
    outs = pl.pallas_call(
        take_kernel,
        out_shape=tuple(shape(rows, local) for rows in parts) * 2,
        in_specs=[pl.BlockSpec(memory_space=pltpu.HBM)],
        out_specs=(VMEM,) * (2 * len(parts)),
        scratch_shapes=[pltpu.SemaphoreType.DMA((2 * len(parts),))],
        name="take",
        cost_estimate=pl.CostEstimate(flops=0, bytes_accessed=4 * tokens.size, transcendentals=0),
        compiler_params=pltpu.CompilerParams(vmem_limit_bytes=4 << 20),
    )(pltpu.with_memory_space_constraint(tokens, pltpu.HBM))
    return outs[: len(parts)], outs[len(parts) :]


def mix_kernel(count, last, toeplitz_ref, *refs):
    sources, refs = refs[:count], refs[count:]
    gate_ref, refs = (refs[0], refs[1:]) if last else (None, refs)
    total_ref, outs = refs[0] if last else None, refs[1:] if last else refs
    heads = toeplitz_ref.shape[0]
    wide = outs[0].shape[1] // heads
    for head in range(heads):
        lanes = slice(head * wide, (head + 1) * wide)
        stacked = jnp.concatenate([source[:, lanes] for source in sources], axis=0)
        mixed = jnp.dot(toeplitz_ref[head], stacked, preferred_element_type=jnp.float32)
        if last:
            mixed += total_ref[:, lanes]
            gate = gate_ref[:, lanes].astype(jnp.float32)
            mixed = gate / (1.0 + jnp.exp(-gate)) * mixed
        mixed = mixed.astype(outs[0].dtype)
        outs[0][:, lanes] = mixed
        start = 0
        for out_ref in outs[1:]:
            out_ref[:, lanes] = mixed[start : start + out_ref.shape[0]]
            start += out_ref.shape[0]


def mix(toeplitz_blocks, sources, total, gating, parts):
    block, local = sources[0].shape
    last = gating is not None
    others = [gating, total] if last else []
    outs = (shape(block, local, dtype=jnp.bfloat16 if last else jnp.float32),)
    outs += tuple(shape(rows, local) for rows in parts)
    return call(
        functools.partial(mix_kernel, len(sources), last),
        outs,
        [VMEM] * (1 + len(sources) + len(others)),
        2 * len(sources) * block * block * local,
        toeplitz_blocks.size * 2 + (len(sources) + 4) * block * local * 2,
    )(toeplitz_blocks, *sources, *others)


def rows_of(refs):
    return refs[0][...] if len(refs) == 1 else jnp.concatenate([ref[...] for ref in refs], axis=0)


def product(own_refs, peer_refs, weight_ref):
    depth = own_refs[0].shape[1]
    chan = lax.axis_index("chan")
    own_rows = weight_ref[pl.ds(pl.multiple_of(chan * depth, depth), depth), :]
    peer_rows = weight_ref[pl.ds(pl.multiple_of((1 - chan) * depth, depth), depth), :]
    total = jnp.dot(rows_of(own_refs), own_rows, preferred_element_type=jnp.float32)
    return total + jnp.dot(rows_of(peer_refs), peer_rows, preferred_element_type=jnp.float32)


def project_kernel(parts, weight_ref, *refs):
    own_refs, peer_refs, out_refs = refs[:parts], refs[parts : 2 * parts], refs[2 * parts :]
    total = product(own_refs, peer_refs, weight_ref)
    wide = total.shape[1] // len(out_refs)
    for at, out_ref in enumerate(out_refs):
        out_ref[...] = total[:, at * wide : (at + 1) * wide].astype(jnp.bfloat16)


def project(own, peer, weight, count):
    block = sum(value.shape[0] for value in own)
    return call(
        functools.partial(project_kernel, len(own)),
        tuple(shape(block, weight.shape[1] // count) for _ in range(count)),
        [VMEM] * (1 + 2 * len(own)),
        2 * block * weight.size,
        2 * weight.size + 4 * block * weight.shape[0],
    )(weight, *own, *peer)


def step_kernel(own_ref, peer_ref, out_own_ref, out_peer_ref, *refs):
    in_ref, first_ref, signal_ref, gate_ref, all_ref = refs
    depth = own_ref.shape[1]
    chan = lax.axis_index("chan")
    at = pl.ds(pl.multiple_of(chan * depth, depth), depth)
    other = pl.ds(pl.multiple_of((1 - chan) * depth, depth), depth)
    all_ref[:, at] = own_ref[...]
    all_ref[:, other] = peer_ref[...]
    gated = all_ref[...]
    first = jnp.dot(gated, out_own_ref[...], preferred_element_type=jnp.float32).astype(jnp.bfloat16)
    second = jnp.dot(gated, out_peer_ref[...], preferred_element_type=jnp.float32).astype(jnp.bfloat16)
    first_ref[...] = first
    all_ref[:, at] = first
    all_ref[:, other] = second
    total = jnp.dot(all_ref[...], in_ref[...], preferred_element_type=jnp.float32)
    signal_ref[...] = total[:, :depth].astype(jnp.bfloat16)
    gate_ref[...] = total[:, depth:].astype(jnp.bfloat16)


def step(own, peer, out_own, out_peer, in_weight):
    block, depth = own.shape
    return pl.pallas_call(
        step_kernel,
        out_shape=(shape(block, depth),) * 3,
        in_specs=[VMEM] * 5,
        out_specs=(VMEM,) * 3,
        scratch_shapes=[pltpu.VMEM((block, 2 * depth), jnp.bfloat16)],
        name="step",
        cost_estimate=pl.CostEstimate(
            flops=16 * block * depth * depth, bytes_accessed=16 * depth * depth + 10 * own.size, transcendentals=0
        ),
        compiler_params=pltpu.CompilerParams(vmem_limit_bytes=12 << 20),
    )(own, peer, out_own, out_peer, in_weight)


def finish_kernel(weight_ref, first_ref, first_home_ref, near_ref, home_ref, own_ref, peer_ref, out_ref, lower_ref, sems):
    section = lax.axis_index("section")
    sequence, _ = position()
    rows = home_ref.shape[0]
    block = near_ref.shape[0]

    def run(copies):
        for copy in copies:
            copy.start()
        return copies

    @pl.when(section == 0)
    def _():
        copies = run(
            [
                pltpu.make_async_copy(first_ref, out_ref.at[0, sequence], sems.at[0]),
                pltpu.make_async_copy(first_home_ref, out_ref.at[0, 1 - sequence], sems.at[1]),
            ]
        )
        for copy in copies:
            copy.wait()

    @pl.when(section == 1)
    def _():
        copies = run(
            [
                pltpu.make_async_copy(near_ref, out_ref.at[0, sequence], sems.at[0]),
                pltpu.make_async_copy(home_ref, out_ref.at[0, 1 - sequence, pl.ds(0, rows), :], sems.at[1]),
            ]
        )
        lower_ref[...] = product([own_ref], [peer_ref], weight_ref).astype(jnp.bfloat16)
        copies += run(
            [pltpu.make_async_copy(lower_ref, out_ref.at[0, 1 - sequence, pl.ds(rows, block - rows), :], sems.at[2])]
        )
        for copy in copies:
            copy.wait()


def finish(weight, first, first_home, near, home, own, peer):
    block, local = first.shape
    return pl.pallas_call(
        finish_kernel,
        out_shape=shape(1, MB, block, local),
        in_specs=[VMEM] * 7,
        out_specs=pl.BlockSpec(memory_space=pltpu.HBM),
        scratch_shapes=[pltpu.VMEM(own.shape, jnp.bfloat16), pltpu.SemaphoreType.DMA((3,))],
        name="finish",
        cost_estimate=pl.CostEstimate(
            flops=block * weight.size, bytes_accessed=weight.size * 2 + 12 * first.size, transcendentals=0
        ),
        compiler_params=pltpu.CompilerParams(vmem_limit_bytes=12 << 20),
    )(weight, first, first_home, near, home, own, peer)


def both_layers(tokens, in_proj, filters, out_proj, widths):
    count = lax.axis_size("seq")
    half = count // 2
    section = lax.axis_index("section")
    block = tokens.shape[1]
    _, _ = position()

    def swap(value, axis):
        return lax.ppermute(value, axis, [(0, 1), (1, 0)])

    def swap_in(value, at):
        return lax.ppermute(value, ("chan", "section"), [(at, 2 + at), (2 + at, at)])

    def across(value, from_section, to_section):
        pairs = [(2 * i + from_section, 2 * ((i + half) % count) + to_section) for i in range(count)]
        return lax.ppermute(value, ("seq", "section"), pairs)

    def pick(zero, one):
        return jnp.where(section == 0, zero, one)

    def where_held(which, held):
        low = held < half
        if which == 0:
            return (held, 0) if low else (held - half, 1)
        return (held + half, 1) if low else (held, 0)

    def ring(value, lag):
        pairs = []
        for which in range(MB):
            for held in range(count):
                source, target = where_held(which, held), where_held(which, (held + lag) % count)
                pairs.append((2 * source[0] + source[1], 2 * target[0] + target[1]))
        return lax.ppermute(value, ("seq", "section"), pairs)

    def halves(value):
        return value[: value.shape[0] // 2], value[value.shape[0] // 2 :]

    def each(move, values):
        moved = []
        for value in values:
            moved.append(move(value))
        return moved

    other_tokens, own_tokens = take(tokens, two_parts(block, LEAVING))
    swapped = each(lambda value: across(value, 1, 1), other_tokens)
    current = [pick(own, moved) for own, moved in zip(own_tokens, swapped)]
    peer = each(lambda value: swap(value, "chan"), current)

    in_near = in_proj[0].reshape(in_proj.shape[1], -1)
    in_far = swap(in_near, "section")
    taps = filters[0]
    far_taps = swap(taps, "section")
    out_near = out_proj[0]
    out_far = swap(out_near, "section")

    groups = GROUPS
    blocks = []
    for layer in range(2):
        blocks.append(toeplitz(layer, widths, taps, far_taps, block, groups))

    def gathered(signal):
        if count != BAND:
            return [ring(signal, lag) if lag else signal for lag in range(-REACH, REACH)]
        near = [signal]
        for apart in range(1, REACH):
            near.append(lax.ppermute(signal, "seq", [(i, i ^ apart) for i in range(count)]))
        return near + each(lambda value: swap(value, "section"), near)

    def mixed(layer, sources, gating, parts):
        total = (None,)
        for group, members in enumerate(groups):
            last = group == len(groups) - 1
            chosen = [sources[slot] for slot in members]
            total = mix(blocks[layer][group], chosen, total[0], gating if last else None, parts if last else ())
        return total

    in_first, in_last = pick(in_near, in_far), pick(in_far, in_near)
    signal, gating = project(current, peer, in_first, 2)
    sources = gathered(signal)

    upper, lower = halves(out_near)[0], halves(out_far)[1]
    sent, _ = lax.optimization_barrier((pick(upper, lower), signal))
    part = swap(sent, "chan")
    other = swap(part, "section")
    out_peer = pick(jnp.concatenate([part, other]), jnp.concatenate([other, part]))
    out_first, out_last = pick(out_near, out_far), pick(out_far, out_near)

    (gated,) = mixed(0, sources, gating, ())
    gated_peer = swap(gated, "chan")
    gated_home = across(gated, 1, 0)
    first, signal, gating = step(gated, gated_peer, out_first, out_peer, in_last)
    sources = gathered(signal)
    home_peer = swap_in(gated_home, 0)
    (first_home,) = project([gated_home], [home_peer], out_first, 1)
    gated, upper, lower = mixed(1, sources, gating, two_parts(block, HOMING))

    upper_peer = swap(upper, "chan")
    lower_home = across(lower, 1, 1)
    near_peer = lax.ppermute(gated, ("chan", "section"), [(0, 3), (2, 1)])
    near_own = swap(gated, "section")
    (second_upper,) = project([upper], [upper_peer], out_last, 1)
    upper_home = across(second_upper, 1, 1)
    (second_near,) = project([near_own], [near_peer], out_last, 1)
    lower_home_peer = swap(lower_home, "chan")
    return finish(out_last, first, first_home, second_near, upper_home, lower_home, lower_home_peer)


def solution(mesh):
    placed = (
        P(None, "seq", "chan"),
        P("section", None, None, "chan"),
        P("section", "chan", None),
        P("section", None, "chan"),
        P(),
    )
    return jax.shard_map(
        both_layers,
        mesh=mesh,
        in_specs=placed,
        out_specs=P("section", None, "seq", "chan"),
        check_vma=False,
    )
```
